32 devices in a mesh: member: 8 (over z, core), basin: 4 (over y, x).
Axes of the slice: x: 2, y: 2, z: 4, core: 2. Of those that a mesh axis runs over, the one named last changes fastest.
Arguments:
- prior_params: float32 [256, 8, 512], P('member', None, 'basin'), may hold values from -3 to 3
- lateral_flow: float32 [256, 2, 65536], P('member', None, 'basin'), may hold values from 0.2 to 2
- inflow_start: float32 [65536], P('basin'), may hold values from 0.5 to 4
- outflow_start: float32 [65536], P('basin'), may hold values from 0.5 to 4
- reach_count: int32 [512], P('basin'), may hold values from 64 to 128
- downstream: int32 [512], P('basin'), may hold values from 0 to 63
- gauge_reach: int32 [2048], P('basin'), may hold values from 0 to 16383
- observed: float32 [2, 2048], P(None, 'basin'), may hold values from 0.5 to 4
- obs_var: float32 [2, 2048], P(None, 'basin'), may hold values from 0.02 to 0.5
- obs_noise: float32 [256, 2, 2048], P('member', None, 'basin'), may hold values from -4 to 4
Outputs:
- posterior: float32 [256, 8, 512], P('member', None, 'basin')
- predicted: float32 [256, 2, 2048], P('member', None, 'basin')
The draws below stay inside these ranges and needn't reach their ends.
All inputs are finite; a program needn't handle non-finite values.
Results may differ from the reference program's by a relative error of at most 0.0003.
Values sent between devices are 32-bit elements; how exact they have to be, the bound alone decides.
A program may use at most 128 MiB of HBM per device.

```python
import math
import jax
import jax.numpy as jnp
from jax import lax

LANES = 128
NPAR = 8
HOURS = 2
M_DEV = 32
BLK_LEV = 64
LEV_DEV = 2
GAUGE_DEV = 512
MEMBERS = 256
LEVELS = 8
BLOCKS = 512
REACHES = 65536
GAUGES = 2048
N_MEMBER = 8


def draw_reach_count(key, part):
    counts = jax.random.randint(key, (BLOCKS,), 64, 129, dtype=jnp.int32)
    return counts.at[0].set(128)


def with_ends(array, key, low, high):
    spot = [jax.random.randint(jax.random.fold_in(key, axis), (), 0, length) for axis, length in enumerate(array.shape)]
    longest = array.shape.index(max(array.shape))
    neighbour = spot[:longest] + [(spot[longest] + 1) % array.shape[longest]] + spot[longest + 1:]
    return array.at[tuple(spot)].set(low).at[tuple(neighbour)].set(high)


def level_of(stream_key, shape, split, least, top_value):
    loudness = 1.0
    for dim, shards_of in split:
        draws = jax.random.uniform(jax.random.fold_in(jax.random.fold_in(stream_key, 6), dim), (shards_of,), jnp.float32, least / len(split), top_value / len(split))
        loudness = loudness * jnp.repeat(jnp.exp(draws), shape[dim] // shards_of).reshape((-1,) + (1,) * (len(shape) - 1 - dim))
    return loudness


def scatter_about(key, shape, deviation, most, shards=(), kind=jnp.bfloat16):
    loudness = level_of(key, shape, shards, -0.22, 0.18) if shards else 1.0
    entries = jax.random.normal(key, shape, jnp.float32) * deviation * loudness
    return jnp.minimum(jnp.maximum(entries, -most), most).astype(kind)


def setup_inputs(seed: int = 0) -> dict:
    seeds = jax.random.split(jax.random.key(seed), 11)
    prior_params = scatter_about(seeds[0], (MEMBERS, NPAR, BLOCKS), 0.7, 3.0, ((0, 8), (2, 4)), jnp.float32)
    lateral_flow = jnp.clip(jnp.exp(math.log(2.0) - 2.3025851 * jax.random.uniform(seeds[1], (MEMBERS, HOURS, REACHES), jnp.float32) ** level_of(seeds[1], (MEMBERS, HOURS, REACHES), ((0, 8), (2, 4)), -0.2, 0.2)), 0.2, 2.0)
    inflow_start = jnp.clip(0.5 + 3.5 * jax.random.uniform(seeds[2], (REACHES,), jnp.float32) ** level_of(seeds[2], (REACHES,), ((0, 4),), -0.2, 0.2), 0.5, 4.0)
    outflow_start = jnp.clip(0.5 + 3.5 * jax.random.uniform(seeds[3], (REACHES,), jnp.float32) ** level_of(seeds[3], (REACHES,), ((0, 4),), -0.2, 0.2), 0.5, 4.0)
    reach_count = draw_reach_count(jax.random.fold_in(seeds[10], 71), 0)
    downstream = with_ends(jax.random.randint(seeds[5], (BLOCKS,), 0, BLK_LEV), jax.random.fold_in(seeds[5], 1), 0, BLK_LEV - 1).astype(jnp.int32)
    gauge_reach = with_ends(jax.random.randint(seeds[6], (GAUGES,), 0, BLK_LEV * LEV_DEV * LANES), jax.random.fold_in(seeds[6], 1), 0, (BLK_LEV * LEV_DEV * LANES) - 1).astype(jnp.int32)
    observed = jnp.clip(0.5 + 3.5 * jax.random.uniform(seeds[7], (HOURS, GAUGES), jnp.float32) ** level_of(seeds[7], (HOURS, GAUGES), ((1, 4),), -0.2, 0.2), 0.5, 4.0)
    obs_var = jnp.clip(jnp.exp(math.log(0.5) - 3.218876 * jax.random.uniform(seeds[8], (HOURS, GAUGES), jnp.float32) ** level_of(seeds[8], (HOURS, GAUGES), ((1, 4),), -0.2, 0.2)), 0.02, 0.5)
    obs_noise = scatter_about(seeds[9], (MEMBERS, HOURS, GAUGES), 1.0, 4.0, ((0, 8), (2, 4)), jnp.float32)
    return dict(prior_params=prior_params, lateral_flow=lateral_flow, inflow_start=inflow_start, outflow_start=outflow_start, reach_count=reach_count, downstream=downstream, gauge_reach=gauge_reach, observed=observed, obs_var=obs_var, obs_noise=obs_noise)


exact_mode = lax.Precision.HIGHEST

def inverse_sinh(values):
    return jnp.log(values + jnp.sqrt(values * values + 1.0))

def route_coefficients(prior_params):
    storage = 0.02 + 0.1 * jax.nn.sigmoid(prior_params[:, 0, :])
    weighting = 0.2 * jax.nn.sigmoid(prior_params[:, 1, :])
    denominator = storage * (1.0 - weighting) + 0.5
    weight_now = (0.5 - storage * weighting) / denominator
    weight_back = (0.5 + storage * weighting) / denominator
    weight_carry = (storage * (1.0 - weighting) - 0.5) / denominator
    return (weight_now[:, :, None], weight_back[:, :, None], weight_carry[:, :, None])

def lateral_scaling(prior_params, lane_count):
    lane_pos = jnp.arange(lane_count, dtype=jnp.float32)
    orders = jnp.arange(6, dtype=jnp.float32)
    cosine_modes = jnp.cos(math.pi * orders[:, None] * (lane_pos[None, :] + 0.5) / lane_count)
    exponent = jnp.einsum('mkb,kr->mbr', 0.2 * prior_params[:, 2:, :], cosine_modes, precision=exact_mode)
    return jnp.exp(exponent)

def solve_gram(gram_matrix, cross_matrix):
    factor = jnp.linalg.cholesky(gram_matrix)
    halfway = lax.linalg.triangular_solve(factor, cross_matrix, left_side=True, lower=True)
    return lax.linalg.triangular_solve(factor, halfway, left_side=True, lower=True, transpose_a=True)

def to_levels(values, group_size):
    shaped = values.reshape((group_size, LEVELS, BLK_LEV) + values.shape[2:])
    return jnp.moveaxis(shaped, 1, 0)

def reference(prior_params, lateral_flow, inflow_start, outflow_start, reach_count, downstream, gauge_reach, observed, obs_var, obs_noise):
    lane_ids = jnp.arange(LANES, dtype=jnp.int32)
    live_mask = (lane_ids[None, :] < reach_count[:, None]).astype(jnp.float32).reshape(LEVELS, BLK_LEV, LANES)
    targets = jnp.arange(BLK_LEV, dtype=jnp.int32)
    one_hot = (downstream.reshape(LEVELS, BLK_LEV)[:, None, :] == targets[None, :, None]).astype(jnp.float32)
    start_in = inflow_start.reshape(LEVELS, BLK_LEV, LANES) * live_mask
    start_out = outflow_start.reshape(LEVELS, BLK_LEV, LANES) * live_mask
    flat_index = jnp.arange(GAUGES, dtype=jnp.int32) // GAUGE_DEV * (BLK_LEV * LEV_DEV * LANES) + gauge_reach

    def one_group(operands):
        prior_group, lateral_group = operands
        group_size = prior_group.shape[0]
        weight_now, weight_back, weight_carry = route_coefficients(prior_group)
        scaling = lateral_scaling(prior_group, LANES)
        now_lev = to_levels(weight_now, group_size)
        back_lev = to_levels(weight_back, group_size)
        carry_lev = to_levels(weight_carry, group_size)
        scale_lev = to_levels(scaling, group_size)
        prev_in = jnp.broadcast_to(start_in[:, None], (LEVELS, group_size, BLK_LEV, LANES))
        prev_out = jnp.broadcast_to(start_out[:, None], (LEVELS, group_size, BLK_LEV, LANES))
        results = []
        for hour_idx in range(HOURS):
            lateral_lev = to_levels(lateral_group[:, hour_idx].reshape(group_size, BLOCKS, LANES), group_size)

            def level_step(upstream, pieces):
                coef_now, coef_back, coef_carry, scale_now, lateral_now, mask_now, hot_now, old_in, old_out = pieces
                inflow = mask_now * (lateral_now * scale_now + upstream)
                outflow = coef_now * inflow + coef_back * old_in + coef_carry * old_out
                downstream_in = jnp.einsum('nj,gjr->gnr', hot_now, outflow, precision=exact_mode)
                return (downstream_in, (inflow, outflow))
            initial = jnp.zeros((group_size, BLK_LEV, LANES), jnp.float32)
            _, (prev_in, prev_out) = lax.scan(level_step, initial, (now_lev, back_lev, carry_lev, scale_lev, lateral_lev, live_mask, one_hot, prev_in, prev_out))
            flat = jnp.moveaxis(prev_out, 0, 1).reshape(group_size, REACHES)
            results.append(inverse_sinh(flat[:, flat_index]))
        return jnp.stack(results, 1)
    grouped = lax.map(one_group, (prior_params.reshape(N_MEMBER, M_DEV, NPAR, BLOCKS), lateral_flow.reshape(N_MEMBER, M_DEV, HOURS, REACHES)))
    predicted = grouped.reshape(MEMBERS, HOURS, GAUGES)
    spread = jnp.sqrt(obs_var)
    spread_root = math.sqrt(MEMBERS - 1.0)
    mean_pred = lax.optimization_barrier(jnp.sum(predicted, 0)) / MEMBERS
    scaled = (predicted - mean_pred) / (spread_root * (2.0 * spread))
    innovation = (observed + 2.0 * spread * obs_noise - predicted) / (2.0 * spread)
    scaled_rows = scaled.reshape(MEMBERS, HOURS * GAUGES)
    innov_rows = innovation.reshape(MEMBERS, HOURS * GAUGES)
    gram_matrix = jnp.dot(scaled_rows.astype(jnp.float32), scaled_rows.T.astype(jnp.float32), precision=exact_mode, preferred_element_type=jnp.float32)
    cross_matrix = jnp.dot(scaled_rows.astype(jnp.float32), innov_rows.T.astype(jnp.float32), precision=exact_mode, preferred_element_type=jnp.float32)
    gram_matrix = gram_matrix + jnp.eye(MEMBERS, dtype=jnp.float32)
    solved = solve_gram(gram_matrix, cross_matrix)
    mean_prior = lax.optimization_barrier(jnp.sum(prior_params, 0)) / MEMBERS
    anomaly = (prior_params - mean_prior) / spread_root
    posterior = prior_params + jnp.einsum('mn,mkb->nkb', solved, anomaly, precision=exact_mode)
    return (posterior, predicted)
```

```python
import functools
import math

import jax
import jax.numpy as jnp
from jax import lax
from jax.experimental import pallas as pl
from jax.experimental.pallas import tpu as pltpu
from jax.sharding import PartitionSpec as P

LANES = 128
BLK_LEV = 64
exact_mode = lax.Precision.HIGHEST
VMEM = pltpu.VMEM
SMEM = pltpu.SMEM
MESH = pl.DeviceIdType.MESH


def vmem_spec():
    return pl.BlockSpec(memory_space=VMEM)


def smem_spec():
    return pl.BlockSpec(memory_space=SMEM)


def exchange_body(axis, n, spread_out, x_ref, o_ref, send_sem, recv_sem, own_sem):
    me = lax.axis_index(axis)
    barrier = pltpu.get_barrier_semaphore()
    for i in range(1, n):
        pl.semaphore_signal(
            barrier, inc=1, device_id={axis: lax.rem(me + i, n)}, device_id_type=MESH
        )
    pl.semaphore_wait(barrier, n - 1)
    copies = []
    for i in range(1, n):
        peer = lax.rem(me + i, n)
        copies.append(
            pltpu.make_async_remote_copy(
                src_ref=x_ref.at[peer] if spread_out else x_ref,
                dst_ref=o_ref.at[me],
                send_sem=send_sem.at[i - 1],
                recv_sem=recv_sem.at[i - 1],
                device_id={axis: peer},
                device_id_type=MESH,
            )
        )
    for copy in copies:
        copy.start()
    own = pltpu.make_async_copy(x_ref.at[me] if spread_out else x_ref, o_ref.at[me], own_sem)
    own.start()
    own.wait()
    for copy in copies:
        copy.wait()


def exchange(x, axis, collective_id, spread_out=False):
    n = lax.axis_size(axis)
    shape = x.shape if spread_out else (n,) + x.shape
    return pl.pallas_call(
        functools.partial(exchange_body, axis, n, spread_out),
        out_shape=jax.ShapeDtypeStruct(shape, x.dtype),
        in_specs=[vmem_spec()],
        out_specs=vmem_spec(),
        scratch_shapes=[
            pltpu.SemaphoreType.DMA((n - 1,)),
            pltpu.SemaphoreType.DMA((n - 1,)),
            pltpu.SemaphoreType.DMA,
        ],
        compiler_params=pltpu.CompilerParams(collective_id=collective_id, has_side_effects=True),
        name=f"exchange_{collective_id}",
    )(x)


def doubling_bits(n):
    bits = []
    bit = n // 2
    while bit:
        bits.append(bit)
        bit //= 2
    return bits


def doubling_body(axis, n, x_ref, o_ref, send_sem, recv_sem, own_sem):
    me = lax.axis_index(axis)
    partners = [me + bit * (1 - 2 * lax.rem(me // bit, 2)) for bit in doubling_bits(n)]
    barrier = pltpu.get_barrier_semaphore()
    for partner in partners:
        pl.semaphore_signal(barrier, inc=1, device_id={axis: partner}, device_id_type=MESH)
    own = pltpu.make_async_copy(x_ref, o_ref.at[0], own_sem)
    own.start()
    own.wait()
    pl.semaphore_wait(barrier, len(partners))
    for k, partner in enumerate(partners):
        held = 2**k
        copy = pltpu.make_async_remote_copy(
            src_ref=o_ref.at[pl.ds(0, held)],
            dst_ref=o_ref.at[pl.ds(held, held)],
            send_sem=send_sem.at[k],
            recv_sem=recv_sem.at[k],
            device_id={axis: partner},
            device_id_type=MESH,
        )
        copy.start()
        copy.wait()


def doubling_gather(x, axis, collective_id):
    n = lax.axis_size(axis)
    steps = len(doubling_bits(n))
    return pl.pallas_call(
        functools.partial(doubling_body, axis, n),
        out_shape=jax.ShapeDtypeStruct((n,) + x.shape, x.dtype),
        in_specs=[vmem_spec()],
        out_specs=vmem_spec(),
        scratch_shapes=[
            pltpu.SemaphoreType.DMA((steps,)),
            pltpu.SemaphoreType.DMA((steps,)),
            pltpu.SemaphoreType.DMA,
        ],
        compiler_params=pltpu.CompilerParams(collective_id=collective_id, has_side_effects=True),
        name=f"doubling_{collective_id}",
    )(x)


def permuted_gather(x, axis):
    n = lax.axis_size(axis)
    held = x[None]
    for bit in doubling_bits(n):
        other = lax.ppermute(held, axis, [(i, i ^ bit) for i in range(n)])
        held = jnp.concatenate([held, other], 0)
    return held


def route_body(
    seg_count, level_count, members, gauges,
    basin_ref, down_ref, count_ref, gauge_ref,
    now_ref, back_ref, carry_ref, par_ref, cos_ref, lat_ref, pin_ref, pout_ref, pick_ref, fold_ref,
    out_ref,
    up_ref, flow_ref, row_ref,
):
    first = basin_ref[0]
    lev = BLK_LEV
    seg_blocks = level_count * lev
    rows = members
    shape = (rows, LANES)
    place = (lax.broadcasted_iota(jnp.int32, shape, 1) // members) * members
    place = place + lax.broadcasted_iota(jnp.int32, shape, 0)
    zero = jnp.zeros(shape, jnp.float32)

    def clear(i, _):
        up_ref[i] = jnp.zeros((2 * rows, LANES), jnp.float32)
        return 0

    def sweep(seg, level, parity, own):
        base = seg * seg_blocks + level * lev

        def block(j, _):
            b = base + j
            here = level * lev + j
            live = place < count_ref[b]
            now = now_ref[pl.ds(b, 1), :]
            back = back_ref[pl.ds(b, 1), :]
            carry = carry_ref[pl.ds(b, 1), :]
            if own:
                expo = cos_ref[0] * par_ref[0, pl.ds(here, 1), :]
                for k in range(1, cos_ref.shape[0]):
                    expo = expo + cos_ref[k] * par_ref[k, pl.ds(here, 1), :]
                scale = jnp.exp(expo)
                add0 = lat_ref[here, 0] * scale
                add1 = lat_ref[here, 1] * scale
                if level > 0:
                    add0 = add0 + up_ref[parity * lev + j, :rows]
                    add1 = add1 + up_ref[parity * lev + j, rows:]
                in0 = jnp.where(live, add0, 0.0)
                in1 = jnp.where(live, add1, 0.0)
                start = back * pin_ref[here] + carry * pout_ref[here]
                out0 = now * in0 + jnp.where(live, start, 0.0)
            else:
                in0 = jnp.where(live, up_ref[parity * lev + j, :rows], 0.0)
                in1 = jnp.where(live, up_ref[parity * lev + j, rows:], 0.0)
                out0 = now * in0
            out1 = now * in1 + back * in0 + carry * out0
            up_ref[parity * lev + j] = jnp.zeros((2 * rows, LANES), jnp.float32)
            flow_ref[pl.ds(here * 2 * rows, rows), :] = out0
            flow_ref[pl.ds(here * 2 * rows + rows, rows), :] = out1
            target = (1 - parity) * lev + down_ref[b]
            up_ref[target, :rows] += out0
            up_ref[target, rows:] += out1
            return 0

        lax.fori_loop(0, lev, block, 0, unroll=4)

    def observe(seg):
        def one(g, _):
            slot = gauge_ref[seg * gauges + g]
            row = (slot // LANES) * (2 * rows) + slot % rows
            row_ref[pl.ds(g, 1), :] = flow_ref[pl.ds(row, 1), :]
            row_ref[pl.ds(gauges + g, 1), :] = flow_ref[pl.ds(row + rows, 1), :]
            return 0

        lax.fori_loop(0, gauges, one, 0, unroll=8)
        pick = pick_ref[seg]
        for h in range(2):
            kept = row_ref[h * gauges : (h + 1) * gauges, :] * pick
            out_ref[seg, h * members : (h + 1) * members, :] = lax.dot_general(
                fold_ref[...], kept, (((1,), (1,)), ((), ())),
                precision=exact_mode, preferred_element_type=jnp.float32,
            )

    lax.fori_loop(0, 2 * lev, clear, 0, unroll=8)

    def nothing(seg, _):
        out_ref[seg] = jnp.zeros(out_ref.shape[1:], jnp.float32)
        return 0

    lax.fori_loop(0, first, nothing, 0)
    for level in range(level_count):
        sweep(first, level, level % 2, True)
    observe(first)

    def later(seg, _):
        for level in range(level_count):
            sweep(seg, level, level % 2, False)
        observe(seg)
        return 0

    lax.fori_loop(first + 1, seg_count, later, 0)


def invert_small(d):
    size = d.shape[0]
    lane = lax.broadcasted_iota(jnp.int32, d.shape, 1)
    sub = lax.broadcasted_iota(jnp.int32, d.shape, 0)
    for j in range(size):
        inv = 1.0 / d[j : j + 1, j : j + 1]
        row = jnp.where(lane[:1] == j, 1.0, d[j : j + 1, :]) * inv
        col = d[:, j : j + 1]
        rest = jnp.where(lane == j, 0.0, d) - col * row
        d = jnp.where(sub == j, row, rest)
    return d


def exact_dot(a, b):
    return jnp.dot(a, b, precision=exact_mode, preferred_element_type=jnp.float32)


def solve_body(n, size, chunk_ref, cross_ref, out_ref, a_ref, l_ref):
    total = n * size
    sub = lax.broadcasted_iota(jnp.int32, (size, total), 0)
    lane = lax.broadcasted_iota(jnp.int32, (size, total), 1)
    for q in range(n):
        rows = chunk_ref[q]
        pieces = [rows[:, (p ^ q) * size : ((p ^ q) + 1) * size] for p in range(n)]
        rows = jnp.concatenate(pieces, axis=1)
        a_ref[q * size : (q + 1) * size, :] = rows + jnp.where(lane == sub + q * size, 1.0, 0.0)
    out_ref[...] = cross_ref[...]
    for k in range(n):
        span = slice(k * size, (k + 1) * size)
        left = (k * size // LANES) * LANES
        inverse = invert_small(a_ref[span, span])
        right = exact_dot(inverse, out_ref[span, :])
        l_ref[...] = a_ref[:, span]
        l_ref[span, :] = jnp.zeros((size, size), jnp.float32)
        column = l_ref[...]
        if k < n - 1:
            top = exact_dot(inverse, a_ref[span, left:])
            a_ref[:, left:] -= exact_dot(column, top)
            a_ref[span, left:] = top
        out_ref[...] -= exact_dot(column, right)
        out_ref[span, :] = right


def inverse_sinh(values):
    return jnp.log(values + jnp.sqrt(values * values + 1.0))


def shards(
    prior_params, lateral_flow, inflow_start, outflow_start, reach_count, downstream,
    gauge_reach, observed, obs_var, obs_noise,
):
    md, param_count, block_dev = prior_params.shape
    hours = lateral_flow.shape[1]
    gauges = gauge_reach.shape[0]
    basins = lax.axis_size("basin")
    n_member = lax.axis_size("member")
    members = md * n_member
    level_count = block_dev // BLK_LEV
    packs = LANES // md
    f32 = jnp.float32

    prior_all = permuted_gather(prior_params, "member").reshape(members, param_count * block_dev)

    meta = jnp.concatenate(
        [
            prior_params[:, :2, :].reshape(md * 2, block_dev),
            downstream.astype(f32)[None],
            reach_count.astype(f32)[None],
            gauge_reach.astype(f32).reshape(-1, block_dev),
        ],
        0,
    )
    extra = -meta.shape[0] % 8
    meta = jnp.concatenate([meta, jnp.zeros((extra, block_dev), f32)], 0)
    meta_all = exchange(meta, "basin", 1)
    pair = meta_all[:, : md * 2].reshape(basins, md, 2, block_dev)
    down_all = meta_all[:, md * 2].reshape(-1).astype(jnp.int32)
    count_all = meta_all[:, md * 2 + 1].reshape(-1).astype(jnp.int32)
    gauge_rows = gauges // block_dev
    gauge_all = (
        meta_all[:, md * 2 + 2 : md * 2 + 2 + gauge_rows].reshape(basins, gauges).astype(jnp.int32)
    )

    storage = 0.02 + 0.1 * jax.nn.sigmoid(pair[:, :, 0])
    weighting = 0.2 * jax.nn.sigmoid(pair[:, :, 1])
    denominator = storage * (1.0 - weighting) + 0.5

    def spread_lanes(values):
        turned = jnp.swapaxes(values, -1, -2)
        return jnp.tile(turned, (1, 1, packs)).reshape(-1, LANES)

    weight_now = spread_lanes((0.5 - storage * weighting) / denominator)
    weight_back = spread_lanes((0.5 + storage * weighting) / denominator)
    weight_carry = spread_lanes((storage * (1.0 - weighting) - 0.5) / denominator)

    modes = param_count - 2
    turned = jnp.transpose(0.2 * prior_params[:, 2:, :], (1, 2, 0))
    turned = jnp.tile(turned, (1, 1, packs))
    lane_pos = jnp.arange(LANES, dtype=f32)
    orders = jnp.arange(modes, dtype=f32)
    cosine = jnp.cos(math.pi * orders[:, None] * (lane_pos[None, :] + 0.5) / LANES)
    cosine = jnp.swapaxes(cosine.reshape(modes, packs, md), 1, 2)
    cosine = jnp.repeat(cosine, md, axis=2)

    lateral = lateral_flow.reshape(md, hours, block_dev, packs, md)
    lateral = jnp.transpose(lateral, (2, 1, 4, 3, 0)).reshape(block_dev, hours, md, LANES)

    def start_state(values):
        shaped = jnp.swapaxes(values.reshape(block_dev, packs, md), 1, 2)
        return jnp.repeat(shaped, md, axis=2)

    phase = jnp.arange(LANES, dtype=jnp.int32) // md
    pick = ((gauge_all % LANES) // md)[:, :, None] == phase[None, None, :]
    fold = (
        jnp.arange(LANES, dtype=jnp.int32)[None, :] % md == jnp.arange(md, dtype=jnp.int32)[:, None]
    )
    basin_idx = lax.axis_index("basin").astype(jnp.int32).reshape(1)

    parts = pl.pallas_call(
        functools.partial(route_body, basins, level_count, md, gauges),
        out_shape=jax.ShapeDtypeStruct((basins, 2 * md, gauges), f32),
        in_specs=[smem_spec()] * 4 + [vmem_spec()] * 10,
        out_specs=vmem_spec(),
        scratch_shapes=[
            VMEM((2 * BLK_LEV, 2 * md, LANES), f32),
            VMEM((block_dev * 2 * md, LANES), f32),
            VMEM((2 * gauges, LANES), f32),
        ],
        cost_estimate=pl.CostEstimate(
            flops=40_000_000, bytes_accessed=60_000_000, transcendentals=0
        ),
        name="route",
    )(
        basin_idx, down_all, count_all, gauge_all.reshape(-1),
        weight_now, weight_back, weight_carry, turned, cosine, lateral,
        start_state(inflow_start), start_state(outflow_start), pick.astype(f32), fold.astype(f32),
    )
    arrived = exchange(parts, "basin", 2, spread_out=True)
    flows = jnp.sum(arrived, 0)
    pred = inverse_sinh(flows).reshape(hours, md, gauges)
    predicted = jnp.swapaxes(pred, 0, 1)
    flat = jnp.concatenate([pred[h] for h in range(hours)], axis=1)
    pred_all = doubling_gather(flat, "member", 3).reshape(members, hours * gauges)

    spread = jnp.sqrt(obs_var).reshape(1, -1)
    spread_root = math.sqrt(members - 1.0)
    noise = jnp.concatenate([obs_noise[:, h] for h in range(hours)], axis=1)
    innovation = (observed.reshape(1, -1) + 2.0 * spread * noise - flat) / (2.0 * spread)
    mean_pred = jnp.sum(pred_all, 0, keepdims=True) / members
    scaled_all = (pred_all - mean_pred) / (spread_root * (2.0 * spread))
    scaled = (flat - mean_pred) / (spread_root * (2.0 * spread))
    both = jnp.concatenate([scaled, innovation], 0)
    part = lax.dot_general(
        both, scaled_all, (((1,), (1,)), ((), ())),
        precision=exact_mode, preferred_element_type=f32,
    )
    summed = jnp.sum(exchange(part, "basin", 4), 0)
    chunks = doubling_gather(summed[:md], "member", 5)
    gain = pl.pallas_call(
        functools.partial(solve_body, n_member, md),
        out_shape=jax.ShapeDtypeStruct((members, md), f32),
        in_specs=[vmem_spec()] * 2,
        out_specs=vmem_spec(),
        scratch_shapes=[VMEM((members, members), f32), VMEM((members, md), f32)],
        cost_estimate=pl.CostEstimate(
            flops=40_000_000, bytes_accessed=60_000_000, transcendentals=0
        ),
        name="solve",
    )(chunks, summed[md:].T)

    mean_prior = jnp.sum(prior_all, 0, keepdims=True) / members
    anomaly = (prior_all - mean_prior) / spread_root
    change = lax.dot_general(
        gain, anomaly, (((0,), (0,)), ((), ())), precision=exact_mode, preferred_element_type=f32
    )
    posterior = prior_params + change.reshape(md, param_count, block_dev)
    return (posterior, predicted)


def solution(mesh):
    return jax.shard_map(
        shards,
        mesh=mesh,
        in_specs=(
            P("member", None, "basin"),
            P("member", None, "basin"),
            P("basin"),
            P("basin"),
            P("basin"),
            P("basin"),
            P("basin"),
            P(None, "basin"),
            P(None, "basin"),
            P("member", None, "basin"),
        ),
        out_specs=(P("member", None, "basin"), P("member", None, "basin")),
        check_vma=False,
    )
```

```python
import functools
import math

import jax
import jax.numpy as jnp
from jax import lax
import numpy as np
from jax.experimental import pallas as pl
from jax.experimental.pallas import tpu as pltpu
from jax.sharding import PartitionSpec as P

LANES = 128
BLK_LEV = 64
exact_mode = lax.Precision.HIGHEST
VMEM = pltpu.VMEM
SMEM = pltpu.SMEM
MESH = pl.DeviceIdType.MESH


def vmem_spec():
    return pl.BlockSpec(memory_space=VMEM)


def smem_spec():
    return pl.BlockSpec(memory_space=SMEM)


def exchange_body(axis, n, spread_out, x_ref, o_ref, send_sem, recv_sem, own_sem):
    me = lax.axis_index(axis)
    barrier = pltpu.get_barrier_semaphore()
    for i in range(1, n):
        pl.semaphore_signal(
            barrier, inc=1, device_id={axis: lax.rem(me + i, n)}, device_id_type=MESH
        )
    pl.semaphore_wait(barrier, n - 1)
    copies = []
    for i in range(1, n):
        peer = lax.rem(me + i, n)
        copies.append(
            pltpu.make_async_remote_copy(
                src_ref=x_ref.at[peer] if spread_out else x_ref,
                dst_ref=o_ref.at[me],
                send_sem=send_sem.at[i - 1],
                recv_sem=recv_sem.at[i - 1],
                device_id={axis: peer},
                device_id_type=MESH,
            )
        )
    for copy in copies:
        copy.start()
    own = pltpu.make_async_copy(x_ref.at[me] if spread_out else x_ref, o_ref.at[me], own_sem)
    own.start()
    own.wait()
    for copy in copies:
        copy.wait()


def exchange(x, axis, collective_id, spread_out=False):
    n = lax.axis_size(axis)
    shape = x.shape if spread_out else (n,) + x.shape
    return pl.pallas_call(
        functools.partial(exchange_body, axis, n, spread_out),
        out_shape=jax.ShapeDtypeStruct(shape, x.dtype),
        in_specs=[vmem_spec()],
        out_specs=vmem_spec(),
        scratch_shapes=[
            pltpu.SemaphoreType.DMA((n - 1,)),
            pltpu.SemaphoreType.DMA((n - 1,)),
            pltpu.SemaphoreType.DMA,
        ],
        compiler_params=pltpu.CompilerParams(collective_id=collective_id, has_side_effects=True),
        name=f"exchange_{collective_id}",
    )(x)


def doubling_bits(n):
    bits = []
    bit = n // 2
    while bit:
        bits.append(bit)
        bit //= 2
    return bits


def doubling_body(axis, n, x_ref, o_ref, send_sem, recv_sem, own_sem):
    me = lax.axis_index(axis)
    partners = [me + bit * (1 - 2 * lax.rem(me // bit, 2)) for bit in doubling_bits(n)]
    barrier = pltpu.get_barrier_semaphore()
    for partner in partners:
        pl.semaphore_signal(barrier, inc=1, device_id={axis: partner}, device_id_type=MESH)
    own = pltpu.make_async_copy(x_ref, o_ref.at[0], own_sem)
    own.start()
    own.wait()
    pl.semaphore_wait(barrier, len(partners))
    for k, partner in enumerate(partners):
        held = 2**k
        copy = pltpu.make_async_remote_copy(
            src_ref=o_ref.at[pl.ds(0, held)],
            dst_ref=o_ref.at[pl.ds(held, held)],
            send_sem=send_sem.at[k],
            recv_sem=recv_sem.at[k],
            device_id={axis: partner},
            device_id_type=MESH,
        )
        copy.start()
        copy.wait()


def doubling_gather(x, axis, collective_id):
    n = lax.axis_size(axis)
    steps = len(doubling_bits(n))
    return pl.pallas_call(
        functools.partial(doubling_body, axis, n),
        out_shape=jax.ShapeDtypeStruct((n,) + x.shape, x.dtype),
        in_specs=[vmem_spec()],
        out_specs=vmem_spec(),
        scratch_shapes=[
            pltpu.SemaphoreType.DMA((steps,)),
            pltpu.SemaphoreType.DMA((steps,)),
            pltpu.SemaphoreType.DMA,
        ],
        compiler_params=pltpu.CompilerParams(collective_id=collective_id, has_side_effects=True),
        name=f"doubling_{collective_id}",
    )(x)


def sum_body(axis, n, x_ref, o_ref, land_ref, sem1, sem2, sem3, sem4):
    me = lax.axis_index(axis)
    barrier = pltpu.get_barrier_semaphore()
    for i in range(1, n):
        pl.semaphore_signal(
            barrier, inc=1, device_id={axis: lax.rem(me + i, n)}, device_id_type=MESH
        )
    pl.semaphore_wait(barrier, n - 1)
    copies = []
    for i in range(1, n):
        peer = lax.rem(me + i, n)
        copies.append(
            pltpu.make_async_remote_copy(
                src_ref=x_ref.at[peer], dst_ref=land_ref.at[i - 1],
                send_sem=sem1.at[i - 1], recv_sem=sem2.at[i - 1],
                device_id={axis: peer}, device_id_type=MESH,
            )
        )
    for copy in copies:
        copy.start()
    for copy in copies:
        copy.wait()
    total = x_ref[me]
    for i in range(1, n):
        total = total + land_ref[i - 1]
    o_ref[me] = total
    copies = []
    for i in range(1, n):
        copies.append(
            pltpu.make_async_remote_copy(
                src_ref=o_ref.at[me], dst_ref=o_ref.at[me],
                send_sem=sem3.at[i - 1], recv_sem=sem4.at[i - 1],
                device_id={axis: lax.rem(me + i, n)}, device_id_type=MESH,
            )
        )
    for copy in copies:
        copy.start()
    for copy in copies:
        copy.wait()


def sum_over(x, axis, collective_id):
    n = lax.axis_size(axis)
    return pl.pallas_call(
        functools.partial(sum_body, axis, n),
        out_shape=jax.ShapeDtypeStruct(x.shape, x.dtype),
        in_specs=[vmem_spec()],
        out_specs=vmem_spec(),
        scratch_shapes=[VMEM((n - 1,) + x.shape[1:], x.dtype)]
        + [pltpu.SemaphoreType.DMA((n - 1,))] * 4,
        compiler_params=pltpu.CompilerParams(collective_id=collective_id, has_side_effects=True),
        name=f"sum_{collective_id}",
    )(x)


def permuted_gather(x, axis):
    n = lax.axis_size(axis)
    held = x[None]
    for bit in doubling_bits(n):
        other = lax.ppermute(held, axis, [(i, i ^ bit) for i in range(n)])
        held = jnp.concatenate([held, other], 0)
    return held


def route_body(
    seg_count, level_count, members, gauges, hours, param_count,
    basin_ref, ints_ref,
    meta_ref, prior_ref, cos_ref, pin_ref, pout_ref, lat_hbm,
    out_ref,
    up_ref, flow_ref, row_ref, now_ref, back_ref, carry_ref, par_ref, raw_ref, ready_ref, sem,
):
    first = basin_ref[0]
    lev = BLK_LEV
    seg_blocks = level_count * lev
    rows = members
    packs = LANES // members
    shape = (rows, LANES)
    lane = lax.broadcasted_iota(jnp.int32, shape, 1)
    place = (lane // members) * members + lax.broadcasted_iota(jnp.int32, shape, 0)

    def fetch(m):
        return pltpu.make_async_copy(lat_hbm.at[m], raw_ref.at[:, m], sem.at[m])

    for m in range(members):
        fetch(m).start()

    def clear(i, _):
        up_ref[i] = jnp.zeros((2 * rows, LANES), jnp.float32)
        return 0

    lax.fori_loop(0, 2 * lev, clear, 0, unroll=8)

    def turned(values):
        return jnp.concatenate([values] * packs, axis=0).T

    def coefficients(seg, _):
        storage = 0.02 + 0.1 * jax.nn.sigmoid(meta_ref[seg, :members, :])
        weighting = 0.2 * jax.nn.sigmoid(meta_ref[seg, members : 2 * members, :])
        den = storage * (1.0 - weighting) + 0.5
        span = pl.ds(pl.multiple_of(seg * seg_blocks, seg_blocks), seg_blocks)
        now_ref[span, :] = turned((0.5 - storage * weighting) / den)
        back_ref[span, :] = turned((0.5 + storage * weighting) / den)
        carry_ref[span, :] = turned((storage * (1.0 - weighting) - 0.5) / den)
        return 0

    lax.fori_loop(first, seg_count, coefficients, 0)
    for k in range(param_count - 2):
        par_ref[k] = turned(0.2 * prior_ref[:, 2 + k, :])
    for m in range(members):
        fetch(m).wait()

    def place_group(tiles):
        flat = jnp.concatenate(tiles, axis=0).T
        strips = [flat[q * rows : (q + 1) * rows] for q in range(packs)]
        made = []
        for i in range(packs):
            total = None
            for q in range(packs):
                shift = ((q - i) * members) % LANES
                piece = pltpu.roll(strips[q], shift, 1) if shift else strips[q]
                total = piece if total is None else jnp.where(lane // members == q, piece, total)
            made.append(total)
        return made

    def relayout(group, _):
        base = group * packs
        for h in range(hours):
            tiles = [raw_ref[(base + i) * hours + h] for i in range(packs)]
            for i, tile in enumerate(place_group(tiles)):
                ready_ref[base + i, h] = tile
        for n, ref in enumerate((pin_ref, pout_ref)):
            tiles = [
                jnp.broadcast_to(ref[pl.ds(base + i, 1), :], shape) for i in range(packs)
            ]
            for i, tile in enumerate(place_group(tiles)):
                ready_ref[base + i, hours + n] = tile
        return 0

    lax.fori_loop(0, seg_blocks // packs, relayout, 0, unroll=2)

    def sweep(seg, level, parity, own):
        def block(j, _):
            here = level * lev + j
            b = seg * seg_blocks + here
            live = place < ints_ref[seg, 1, here]
            now = now_ref[pl.ds(b, 1), :]
            back = back_ref[pl.ds(b, 1), :]
            carry = carry_ref[pl.ds(b, 1), :]
            if own:
                expo = cos_ref[0] * par_ref[0, pl.ds(here, 1), :]
                for k in range(1, cos_ref.shape[0]):
                    expo = expo + cos_ref[k] * par_ref[k, pl.ds(here, 1), :]
                scale = jnp.exp(expo)
                add0 = ready_ref[here, 0] * scale
                add1 = ready_ref[here, 1] * scale
                if level > 0:
                    add0 = add0 + up_ref[parity * lev + j, :rows]
                    add1 = add1 + up_ref[parity * lev + j, rows:]
                in0 = jnp.where(live, add0, 0.0)
                in1 = jnp.where(live, add1, 0.0)
                start = back * ready_ref[here, 2] + carry * ready_ref[here, 3]
                out0 = now * in0 + jnp.where(live, start, 0.0)
            else:
                in0 = jnp.where(live, up_ref[parity * lev + j, :rows], 0.0)
                in1 = jnp.where(live, up_ref[parity * lev + j, rows:], 0.0)
                out0 = now * in0
            out1 = now * in1 + back * in0 + carry * out0
            up_ref[parity * lev + j] = jnp.zeros((2 * rows, LANES), jnp.float32)
            flow_ref[pl.ds(here * 2 * rows, rows), :] = out0
            flow_ref[pl.ds(here * 2 * rows + rows, rows), :] = out1
            target = (1 - parity) * lev + ints_ref[seg, 0, here]
            up_ref[target, :rows] += out0
            up_ref[target, rows:] += out1
            return 0

        lax.fori_loop(0, lev, block, 0, unroll=4)

    fold = lax.broadcasted_iota(jnp.int32, shape, 0) == lane % members
    fold = fold.astype(jnp.float32)
    one_lane = lax.broadcasted_iota(jnp.int32, (1, LANES), 1) // members

    def observe(seg):
        def one(g, _):
            slot = ints_ref[seg, 2 + g // LANES, g % LANES]
            row = (slot // LANES) * (2 * rows) + slot % rows
            keep = one_lane == (slot % LANES) // rows
            row_ref[pl.ds(g, 1), :] = jnp.where(keep, flow_ref[pl.ds(row, 1), :], 0.0)
            row_ref[pl.ds(gauges + g, 1), :] = jnp.where(
                keep, flow_ref[pl.ds(row + rows, 1), :], 0.0
            )
            return 0

        lax.fori_loop(0, gauges, one, 0, unroll=8)
        for h in range(2):
            out_ref[seg, h * members : (h + 1) * members, :] = lax.dot_general(
                fold, row_ref[h * gauges : (h + 1) * gauges, :], (((1,), (1,)), ((), ())),
                precision=exact_mode, preferred_element_type=jnp.float32,
            )

    def nothing(seg, _):
        out_ref[seg] = jnp.zeros(out_ref.shape[1:], jnp.float32)
        return 0

    lax.fori_loop(0, first, nothing, 0)
    for level in range(level_count):
        sweep(first, level, level % 2, True)
    observe(first)

    def later(seg, _):
        for level in range(level_count):
            sweep(seg, level, level % 2, False)
        observe(seg)
        return 0

    lax.fori_loop(first + 1, seg_count, later, 0)


def invert_small(d):
    size = d.shape[0]
    lane = lax.broadcasted_iota(jnp.int32, d.shape, 1)
    sub = lax.broadcasted_iota(jnp.int32, d.shape, 0)
    for j in range(0, size, 2):
        i = j + 1
        row0, row1 = d[j : j + 1, :], d[i : i + 1, :]
        col0, col1 = d[:, j : j + 1], d[:, i : i + 1]
        a, b = d[j : j + 1, j : j + 1], d[j : j + 1, i : i + 1]
        e, f = d[i : i + 1, j : j + 1], d[i : i + 1, i : i + 1]
        inv = 1.0 / (a * f - b * e)
        at0, at1 = lane[:1] == j, lane[:1] == i
        row0 = jnp.where(at0, 1.0, jnp.where(at1, 0.0, row0))
        row1 = jnp.where(at0, 0.0, jnp.where(at1, 1.0, row1))
        new0 = (f * row0 - b * row1) * inv
        new1 = (a * row1 - e * row0) * inv
        kept = jnp.where((lane == j) | (lane == i), 0.0, d)
        rest = kept - (col0 * new0 + col1 * new1)
        d = jnp.where(sub == j, new0, jnp.where(sub == i, new1, rest))
    return d


def exact_dot(a, b):
    return jnp.dot(a, b, precision=exact_mode, preferred_element_type=jnp.float32)


def solve_body(n, size, sums_ref, out_ref, a_ref, l_ref):
    total = n * size
    sub = lax.broadcasted_iota(jnp.int32, (total, total), 0)
    lane = lax.broadcasted_iota(jnp.int32, (total, total), 1)
    a_ref[...] = sums_ref[:total, :] + jnp.where(lane == sub, 1.0, 0.0)
    out_ref[...] = sums_ref[total : total + size, :].T
    for k in range(n):
        span = slice(k * size, (k + 1) * size)
        left = (k * size // LANES) * LANES
        inverse = invert_small(a_ref[span, span])
        right = exact_dot(inverse, out_ref[span, :])
        l_ref[...] = a_ref[:, span]
        l_ref[span, :] = jnp.zeros((size, size), jnp.float32)
        column = l_ref[...]
        if k < n - 1:
            top = exact_dot(inverse, a_ref[span, left:])
            a_ref[:, left:] -= exact_dot(column, top)
            a_ref[span, left:] = top
        out_ref[...] -= exact_dot(column, right)
        out_ref[span, :] = right


def inverse_sinh(values):
    return jnp.log(values + jnp.sqrt(values * values + 1.0))


def shards(
    prior_params, lateral_flow, inflow_start, outflow_start, reach_count, downstream,
    gauge_reach, observed, obs_var, obs_noise,
):
    md, param_count, block_dev = prior_params.shape
    hours = lateral_flow.shape[1]
    gauges = gauge_reach.shape[0]
    basins = lax.axis_size("basin")
    n_member = lax.axis_size("member")
    members = md * n_member
    level_count = block_dev // BLK_LEV
    packs = LANES // md
    f32 = jnp.float32

    prior_all = permuted_gather(prior_params, "member").reshape(members, param_count * block_dev)

    gauge_rows = gauges // block_dev
    extra = -(md * 2 + 2 + gauge_rows) % 8
    meta = jnp.concatenate(
        [
            prior_params[:, 0, :],
            prior_params[:, 1, :],
            downstream.astype(f32)[None],
            reach_count.astype(f32)[None],
            gauge_reach.astype(f32).reshape(-1, block_dev),
            jnp.zeros((extra, block_dev), f32),
        ],
        0,
    )
    meta_all = exchange(meta, "basin", 1)
    ints_all = meta_all[:, md * 2 : md * 2 + 2 + gauge_rows].astype(jnp.int32)

    modes = param_count - 2
    lane_pos = np.arange(LANES)
    cosine = np.cos(math.pi * np.arange(modes)[:, None] * (lane_pos[None, :] + 0.5) / LANES)
    cosine = np.swapaxes(cosine.reshape(modes, packs, md), 1, 2)
    cosine = jnp.asarray(np.repeat(cosine, md, axis=2), f32)

    lateral = lateral_flow.reshape(md, hours, block_dev, LANES)
    lateral = jnp.swapaxes(lateral, 1, 2).reshape(md, block_dev * hours, LANES)
    basin_idx = lax.axis_index("basin").astype(jnp.int32).reshape(1)
    seg_coef = VMEM((basins * block_dev, LANES), f32)

    parts = pl.pallas_call(
        functools.partial(route_body, basins, level_count, md, gauges, hours, param_count),
        out_shape=jax.ShapeDtypeStruct((basins, 2 * md, gauges), f32),
        in_specs=[smem_spec()] * 2 + [vmem_spec()] * 5 + [pl.BlockSpec(memory_space=pl.ANY)],
        out_specs=vmem_spec(),
        scratch_shapes=[
            VMEM((2 * BLK_LEV, 2 * md, LANES), f32),
            VMEM((block_dev * 2 * md, LANES), f32),
            VMEM((2 * gauges, LANES), f32),
            seg_coef,
            seg_coef,
            seg_coef,
            VMEM((modes, block_dev, LANES), f32),
            VMEM((block_dev * hours, md, LANES), f32),
            VMEM((block_dev, hours + 2, md, LANES), f32),
            pltpu.SemaphoreType.DMA((md,)),
        ],
        cost_estimate=pl.CostEstimate(
            flops=40_000_000, bytes_accessed=60_000_000, transcendentals=0
        ),
        name="route",
    )(
        basin_idx, ints_all, meta_all, prior_params, cosine,
        inflow_start.reshape(block_dev, LANES), outflow_start.reshape(block_dev, LANES), lateral,
    )
    arrived = exchange(parts, "basin", 2, spread_out=True)
    flows = jnp.sum(arrived, 0)
    pred = inverse_sinh(flows).reshape(hours, md, gauges)
    predicted = jnp.swapaxes(pred, 0, 1)
    flat = jnp.concatenate([pred[h] for h in range(hours)], axis=1)
    pred_all = doubling_gather(flat, "member", 3).reshape(members, hours * gauges)

    spread = jnp.sqrt(obs_var).reshape(1, -1)
    spread_root = math.sqrt(members - 1.0)
    noise = jnp.concatenate([obs_noise[:, h] for h in range(hours)], axis=1)
    innovation = (observed.reshape(1, -1) + 2.0 * spread * noise - flat) / (2.0 * spread)
    mean_pred = jnp.sum(pred_all, 0, keepdims=True) / members
    scaled_all = (pred_all - mean_pred) / (spread_root * (2.0 * spread))
    row_count = members + md
    extra = -row_count % (8 * basins)
    both = jnp.concatenate([scaled_all, innovation, jnp.zeros((extra, flat.shape[1]), f32)], 0)
    part = lax.dot_general(
        both, scaled_all, (((1,), (1,)), ((), ())),
        precision=exact_mode, preferred_element_type=f32,
    )
    sums = sum_over(part.reshape(basins, -1, members), "basin", 4).reshape(-1, members)
    gain = pl.pallas_call(
        functools.partial(solve_body, n_member, md),
        out_shape=jax.ShapeDtypeStruct((members, md), f32),
        in_specs=[vmem_spec()],
        out_specs=vmem_spec(),
        scratch_shapes=[VMEM((members, members), f32), VMEM((members, md), f32)],
        cost_estimate=pl.CostEstimate(
            flops=40_000_000, bytes_accessed=60_000_000, transcendentals=0
        ),
        name="solve",
    )(sums)

    mean_prior = jnp.sum(prior_all, 0, keepdims=True) / members
    anomaly = (prior_all - mean_prior) / spread_root
    change = lax.dot_general(
        gain, anomaly, (((0,), (0,)), ((), ())), precision=exact_mode, preferred_element_type=f32
    )
    posterior = prior_params + change.reshape(md, param_count, block_dev)
    return (posterior, predicted)


def solution(mesh):
    return jax.shard_map(
        shards,
        mesh=mesh,
        in_specs=(
            P("member", None, "basin"),
            P("member", None, "basin"),
            P("basin"),
            P("basin"),
            P("basin"),
            P("basin"),
            P("basin"),
            P(None, "basin"),
            P(None, "basin"),
            P("member", None, "basin"),
        ),
        out_specs=(P("member", None, "basin"), P("member", None, "basin")),
        check_vma=False,
    )
```

```python
import functools
import math

import jax
import jax.numpy as jnp
from jax import lax
import numpy as np
from jax.experimental import pallas as pl
from jax.experimental.pallas import tpu as pltpu
from jax.sharding import PartitionSpec as P

LANES = 128
BLK_LEV = 64
exact_mode = lax.Precision.HIGHEST
VMEM = pltpu.VMEM
SMEM = pltpu.SMEM
MESH = pl.DeviceIdType.MESH


def vmem_spec():
    return pl.BlockSpec(memory_space=VMEM)


def smem_spec():
    return pl.BlockSpec(memory_space=SMEM)


def exchange_body(axis, n, spread_out, x_ref, o_ref, send_sem, recv_sem, own_sem):
    me = lax.axis_index(axis)
    barrier = pltpu.get_barrier_semaphore()
    for i in range(1, n):
        pl.semaphore_signal(
            barrier, inc=1, device_id={axis: lax.rem(me + i, n)}, device_id_type=MESH
        )
    pl.semaphore_wait(barrier, n - 1)
    copies = []
    for i in range(1, n):
        peer = lax.rem(me + i, n)
        copies.append(
            pltpu.make_async_remote_copy(
                src_ref=x_ref.at[peer] if spread_out else x_ref,
                dst_ref=o_ref.at[me],
                send_sem=send_sem.at[i - 1],
                recv_sem=recv_sem.at[i - 1],
                device_id={axis: peer},
                device_id_type=MESH,
            )
        )
    for copy in copies:
        copy.start()
    own = pltpu.make_async_copy(x_ref.at[me] if spread_out else x_ref, o_ref.at[me], own_sem)
    own.start()
    own.wait()
    for copy in copies:
        copy.wait()


def exchange(x, axis, collective_id, spread_out=False):
    n = lax.axis_size(axis)
    shape = x.shape if spread_out else (n,) + x.shape
    return pl.pallas_call(
        functools.partial(exchange_body, axis, n, spread_out),
        out_shape=jax.ShapeDtypeStruct(shape, x.dtype),
        in_specs=[vmem_spec()],
        out_specs=vmem_spec(),
        scratch_shapes=[
            pltpu.SemaphoreType.DMA((n - 1,)),
            pltpu.SemaphoreType.DMA((n - 1,)),
            pltpu.SemaphoreType.DMA,
        ],
        compiler_params=pltpu.CompilerParams(collective_id=collective_id, has_side_effects=True),
        name=f"exchange_{collective_id}",
    )(x)


def doubling_bits(n):
    bits = []
    bit = n // 2
    while bit:
        bits.append(bit)
        bit //= 2
    return bits


def doubling_body(axis, n, x_ref, o_ref, send_sem, recv_sem, own_sem):
    me = lax.axis_index(axis)
    partners = [me + bit * (1 - 2 * lax.rem(me // bit, 2)) for bit in doubling_bits(n)]
    barrier = pltpu.get_barrier_semaphore()
    for partner in partners:
        pl.semaphore_signal(barrier, inc=1, device_id={axis: partner}, device_id_type=MESH)
    own = pltpu.make_async_copy(x_ref, o_ref.at[0], own_sem)
    own.start()
    own.wait()
    pl.semaphore_wait(barrier, len(partners))
    for k, partner in enumerate(partners):
        held = 2**k
        copy = pltpu.make_async_remote_copy(
            src_ref=o_ref.at[pl.ds(0, held)],
            dst_ref=o_ref.at[pl.ds(held, held)],
            send_sem=send_sem.at[k],
            recv_sem=recv_sem.at[k],
            device_id={axis: partner},
            device_id_type=MESH,
        )
        copy.start()
        copy.wait()


def doubling_gather(x, axis, collective_id):
    n = lax.axis_size(axis)
    steps = len(doubling_bits(n))
    return pl.pallas_call(
        functools.partial(doubling_body, axis, n),
        out_shape=jax.ShapeDtypeStruct((n,) + x.shape, x.dtype),
        in_specs=[vmem_spec()],
        out_specs=vmem_spec(),
        scratch_shapes=[
            pltpu.SemaphoreType.DMA((steps,)),
            pltpu.SemaphoreType.DMA((steps,)),
            pltpu.SemaphoreType.DMA,
        ],
        compiler_params=pltpu.CompilerParams(collective_id=collective_id, has_side_effects=True),
        name=f"doubling_{collective_id}",
    )(x)


def sum_body(axis, n, x_ref, o_ref, land_ref, sem1, sem2, sem3, sem4):
    me = lax.axis_index(axis)
    barrier = pltpu.get_barrier_semaphore()
    for i in range(1, n):
        pl.semaphore_signal(
            barrier, inc=1, device_id={axis: lax.rem(me + i, n)}, device_id_type=MESH
        )
    pl.semaphore_wait(barrier, n - 1)
    copies = []
    for i in range(1, n):
        peer = lax.rem(me + i, n)
        copies.append(
            pltpu.make_async_remote_copy(
                src_ref=x_ref.at[peer], dst_ref=land_ref.at[i - 1],
                send_sem=sem1.at[i - 1], recv_sem=sem2.at[i - 1],
                device_id={axis: peer}, device_id_type=MESH,
            )
        )
    for copy in copies:
        copy.start()
    for copy in copies:
        copy.wait()
    total = x_ref[me]
    for i in range(1, n):
        total = total + land_ref[i - 1]
    o_ref[me] = total
    copies = []
    for i in range(1, n):
        copies.append(
            pltpu.make_async_remote_copy(
                src_ref=o_ref.at[me], dst_ref=o_ref.at[me],
                send_sem=sem3.at[i - 1], recv_sem=sem4.at[i - 1],
                device_id={axis: lax.rem(me + i, n)}, device_id_type=MESH,
            )
        )
    for copy in copies:
        copy.start()
    for copy in copies:
        copy.wait()


def sum_over(x, axis, collective_id):
    n = lax.axis_size(axis)
    return pl.pallas_call(
        functools.partial(sum_body, axis, n),
        out_shape=jax.ShapeDtypeStruct(x.shape, x.dtype),
        in_specs=[vmem_spec()],
        out_specs=vmem_spec(),
        scratch_shapes=[VMEM((n - 1,) + x.shape[1:], x.dtype)]
        + [pltpu.SemaphoreType.DMA((n - 1,))] * 4,
        compiler_params=pltpu.CompilerParams(collective_id=collective_id, has_side_effects=True),
        name=f"sum_{collective_id}",
    )(x)


def permuted_step(held, axis, bit):
    n = lax.axis_size(axis)
    other = lax.ppermute(held, axis, [(i, i ^ bit) for i in range(n)])
    return jnp.concatenate([held, other], 0)


def route_body(
    seg_count, level_count, members, gauges, hours, param_count,
    basin_ref, down_ref, count_ref, gauge_row_ref, gauge_pack_ref,
    meta_ref, prior_ref, cos_ref, pin_ref, pout_ref, lat_hbm,
    out_ref,
    up_ref, flow_ref, row_ref, now_ref, back_ref, carry_ref, par_ref, raw_ref, ready_ref, sem,
):
    first = basin_ref[0]
    lev = BLK_LEV
    seg_blocks = level_count * lev
    rows = members
    packs = LANES // members
    shape = (rows, LANES)
    lane = lax.broadcasted_iota(jnp.int32, shape, 1)
    place = (lane // members) * members + lax.broadcasted_iota(jnp.int32, shape, 0)

    def fetch(m):
        return pltpu.make_async_copy(lat_hbm.at[m], raw_ref.at[:, m], sem.at[m])

    for m in range(members):
        fetch(m).start()

    def clear(i, _):
        up_ref[i] = jnp.zeros((2 * rows, LANES), jnp.float32)
        return 0

    lax.fori_loop(0, 2 * lev, clear, 0, unroll=8)

    def turned(values):
        return jnp.concatenate([values] * packs, axis=0).T

    def coefficients(seg, _):
        storage = 0.02 + 0.1 * jax.nn.sigmoid(meta_ref[seg, :members, :])
        weighting = 0.2 * jax.nn.sigmoid(meta_ref[seg, members : 2 * members, :])
        den = storage * (1.0 - weighting) + 0.5
        span = pl.ds(pl.multiple_of(seg * seg_blocks, seg_blocks), seg_blocks)
        now_ref[span, :] = turned((0.5 - storage * weighting) / den)
        back_ref[span, :] = turned((0.5 + storage * weighting) / den)
        carry_ref[span, :] = turned((storage * (1.0 - weighting) - 0.5) / den)
        return 0

    lax.fori_loop(first, seg_count, coefficients, 0)
    for k in range(param_count - 2):
        par_ref[k] = turned(0.2 * prior_ref[:, 2 + k, :])
    for m in range(members):
        fetch(m).wait()

    def place_group(tiles):
        flat = jnp.concatenate(tiles, axis=0).T
        strips = [flat[q * rows : (q + 1) * rows] for q in range(packs)]
        made = []
        for i in range(packs):
            total = None
            for q in range(packs):
                shift = ((q - i) * members) % LANES
                piece = pltpu.roll(strips[q], shift, 1) if shift else strips[q]
                total = piece if total is None else jnp.where(lane // members == q, piece, total)
            made.append(total)
        return made

    def relayout(group, _):
        base = group * packs
        for h in range(hours):
            tiles = [raw_ref[(base + i) * hours + h] for i in range(packs)]
            for i, tile in enumerate(place_group(tiles)):
                ready_ref[base + i, h] = tile
        for n, ref in enumerate((pin_ref, pout_ref)):
            tiles = [
                jnp.broadcast_to(ref[pl.ds(base + i, 1), :], shape) for i in range(packs)
            ]
            for i, tile in enumerate(place_group(tiles)):
                ready_ref[base + i, hours + n] = tile
        return 0

    lax.fori_loop(0, seg_blocks // packs, relayout, 0, unroll=2)

    def sweep(seg, level, parity, own):
        def block(j, _):
            here = level * lev + j
            b = seg * seg_blocks + here
            live = place < count_ref[b]
            now = now_ref[pl.ds(b, 1), :]
            back = back_ref[pl.ds(b, 1), :]
            carry = carry_ref[pl.ds(b, 1), :]
            if own:
                expo = cos_ref[0] * par_ref[0, pl.ds(here, 1), :]
                for k in range(1, cos_ref.shape[0]):
                    expo = expo + cos_ref[k] * par_ref[k, pl.ds(here, 1), :]
                scale = jnp.exp(expo)
                add0 = ready_ref[here, 0] * scale
                add1 = ready_ref[here, 1] * scale
                if level > 0:
                    add0 = add0 + up_ref[parity * lev + j, :rows]
                    add1 = add1 + up_ref[parity * lev + j, rows:]
                in0 = jnp.where(live, add0, 0.0)
                in1 = jnp.where(live, add1, 0.0)
                start = back * ready_ref[here, 2] + carry * ready_ref[here, 3]
                out0 = now * in0 + jnp.where(live, start, 0.0)
            else:
                in0 = jnp.where(live, up_ref[parity * lev + j, :rows], 0.0)
                in1 = jnp.where(live, up_ref[parity * lev + j, rows:], 0.0)
                out0 = now * in0
            out1 = now * in1 + back * in0 + carry * out0
            up_ref[parity * lev + j] = jnp.zeros((2 * rows, LANES), jnp.float32)
            flow_ref[pl.ds(here * 2 * rows, rows), :] = out0
            flow_ref[pl.ds(here * 2 * rows + rows, rows), :] = out1
            target = (1 - parity) * lev + down_ref[b]
            up_ref[target, :rows] += out0
            up_ref[target, rows:] += out1
            return 0

        lax.fori_loop(0, lev, block, 0, unroll=4)

    fold = lax.broadcasted_iota(jnp.int32, shape, 0) == lane % members
    fold = fold.astype(jnp.float32)
    one_lane = lax.broadcasted_iota(jnp.int32, (1, LANES), 1) // members

    def observe(seg):
        first_gauge = seg * gauges

        def one(g, _):
            row = gauge_row_ref[first_gauge + g]
            keep = one_lane == gauge_pack_ref[first_gauge + g]
            row_ref[pl.ds(g, 1), :] = jnp.where(keep, flow_ref[pl.ds(row, 1), :], 0.0)
            row_ref[pl.ds(gauges + g, 1), :] = jnp.where(
                keep, flow_ref[pl.ds(row + rows, 1), :], 0.0
            )
            return 0

        lax.fori_loop(0, gauges, one, 0, unroll=8)
        for h in range(2):
            out_ref[seg, h * members : (h + 1) * members, :] = lax.dot_general(
                fold, row_ref[h * gauges : (h + 1) * gauges, :], (((1,), (1,)), ((), ())),
                precision=exact_mode, preferred_element_type=jnp.float32,
            )

    def nothing(seg, _):
        out_ref[seg] = jnp.zeros(out_ref.shape[1:], jnp.float32)
        return 0

    lax.fori_loop(0, first, nothing, 0)
    for level in range(level_count):
        sweep(first, level, level % 2, True)
    observe(first)

    def later(seg, _):
        for level in range(level_count):
            sweep(seg, level, level % 2, False)
        observe(seg)
        return 0

    lax.fori_loop(first + 1, seg_count, later, 0)


def invert_small(d, panel=8):
    size = d.shape[0]
    lane = lax.broadcasted_iota(jnp.int32, d.shape, 1)
    sub = lax.broadcasted_iota(jnp.int32, d.shape, 0)
    for base in range(0, size, panel):
        cols = [jnp.broadcast_to(d[:, base + i : base + i + 1], d.shape) for i in range(panel)]
        for i in range(panel):
            j = base + i
            pivot = cols[i]
            inv = 1.0 / pivot[j : j + 1, :]
            row = jnp.where(lane[:1] == j, 1.0, d[j : j + 1, :]) * inv
            d = jnp.where(sub == j, row, jnp.where(lane == j, 0.0, d) - pivot * row)
            for l in range(i + 1, panel):
                factor = pivot[base + l : base + l + 1, :] * inv
                cols[l] = jnp.where(sub == j, factor, cols[l] - pivot * factor)
    return d


def exact_dot(a, b):
    return jnp.dot(a, b, precision=exact_mode, preferred_element_type=jnp.float32)


def solve_body(n, size, sums_ref, out_ref, a_ref, l_ref):
    total = n * size
    sub = lax.broadcasted_iota(jnp.int32, (total, total), 0)
    lane = lax.broadcasted_iota(jnp.int32, (total, total), 1)
    a_ref[...] = sums_ref[:total, :] + jnp.where(lane == sub, 1.0, 0.0)
    out_ref[...] = sums_ref[total : total + size, :].T
    for k in range(n):
        span = slice(k * size, (k + 1) * size)
        left = (k * size // LANES) * LANES
        inverse = invert_small(a_ref[span, span])
        right = exact_dot(inverse, out_ref[span, :])
        l_ref[...] = a_ref[:, span]
        l_ref[span, :] = jnp.zeros((size, size), jnp.float32)
        column = l_ref[...]
        if k < n - 1:
            top = exact_dot(inverse, a_ref[span, left:])
            a_ref[:, left:] -= exact_dot(column, top)
            a_ref[span, left:] = top
        out_ref[...] -= exact_dot(column, right)
        out_ref[span, :] = right


def inverse_sinh(values):
    return jnp.log(values + jnp.sqrt(values * values + 1.0))


def shards(
    prior_params, lateral_flow, inflow_start, outflow_start, reach_count, downstream,
    gauge_reach, observed, obs_var, obs_noise,
):
    md, param_count, block_dev = prior_params.shape
    hours = lateral_flow.shape[1]
    gauges = gauge_reach.shape[0]
    basins = lax.axis_size("basin")
    n_member = lax.axis_size("member")
    members = md * n_member
    level_count = block_dev // BLK_LEV
    packs = LANES // md
    f32 = jnp.float32

    prior_steps = doubling_bits(n_member)
    held = permuted_step(prior_params[None], "member", prior_steps[0])

    gauge_rows = gauges // block_dev
    extra = -(md * 2 + 2 + gauge_rows) % 8
    meta = jnp.concatenate(
        [
            prior_params[:, 0, :],
            prior_params[:, 1, :],
            downstream.astype(f32)[None],
            reach_count.astype(f32)[None],
            gauge_reach.astype(f32).reshape(-1, block_dev),
            jnp.zeros((extra, block_dev), f32),
        ],
        0,
    )
    meta_all = exchange(meta, "basin", 1)
    down_all = meta_all[:, md * 2].reshape(-1).astype(jnp.int32)
    count_all = meta_all[:, md * 2 + 1].reshape(-1).astype(jnp.int32)
    slots = meta_all[:, md * 2 + 2 : md * 2 + 2 + gauge_rows].reshape(-1).astype(jnp.int32)
    gauge_row = slots // LANES * (hours * md) + slots % md
    gauge_pack = slots % LANES // md

    modes = param_count - 2
    lane_pos = np.arange(LANES)
    cosine = np.cos(math.pi * np.arange(modes)[:, None] * (lane_pos[None, :] + 0.5) / LANES)
    cosine = np.swapaxes(cosine.reshape(modes, packs, md), 1, 2)
    cosine = jnp.asarray(np.repeat(cosine, md, axis=2), f32)

    lateral = lateral_flow.reshape(md, hours, block_dev, LANES)
    lateral = jnp.swapaxes(lateral, 1, 2).reshape(md, block_dev * hours, LANES)
    held, meta_all = lax.optimization_barrier((held, meta_all))
    for bit in prior_steps[1:-1]:
        held = permuted_step(held, "member", bit)
    basin_idx = lax.axis_index("basin").astype(jnp.int32).reshape(1)
    seg_coef = VMEM((basins * block_dev, LANES), f32)

    parts = pl.pallas_call(
        functools.partial(route_body, basins, level_count, md, gauges, hours, param_count),
        out_shape=jax.ShapeDtypeStruct((basins, 2 * md, gauges), f32),
        in_specs=[smem_spec()] * 5 + [vmem_spec()] * 5 + [pl.BlockSpec(memory_space=pl.ANY)],
        out_specs=vmem_spec(),
        scratch_shapes=[
            VMEM((2 * BLK_LEV, 2 * md, LANES), f32),
            VMEM((block_dev * 2 * md, LANES), f32),
            VMEM((2 * gauges, LANES), f32),
            seg_coef,
            seg_coef,
            seg_coef,
            VMEM((modes, block_dev, LANES), f32),
            VMEM((block_dev * hours, md, LANES), f32),
            VMEM((block_dev, hours + 2, md, LANES), f32),
            pltpu.SemaphoreType.DMA((md,)),
        ],
        cost_estimate=pl.CostEstimate(
            flops=40_000_000, bytes_accessed=60_000_000, transcendentals=0
        ),
        name="route",
    )(
        basin_idx, down_all, count_all, gauge_row, gauge_pack, meta_all, prior_params, cosine,
        inflow_start.reshape(block_dev, LANES), outflow_start.reshape(block_dev, LANES), lateral,
    )
    parts, held = lax.optimization_barrier((parts, held))
    held = permuted_step(held, "member", prior_steps[-1])
    prior_all = held.reshape(members, param_count * block_dev)
    arrived = exchange(parts, "basin", 2, spread_out=True)
    flows = jnp.sum(arrived, 0)
    pred = inverse_sinh(flows).reshape(hours, md, gauges)
    predicted = jnp.swapaxes(pred, 0, 1)
    flat = jnp.concatenate([pred[h] for h in range(hours)], axis=1)
    pred_all = doubling_gather(flat, "member", 3).reshape(members, hours * gauges)

    spread = jnp.sqrt(obs_var).reshape(1, -1)
    spread_root = math.sqrt(members - 1.0)
    noise = jnp.concatenate([obs_noise[:, h] for h in range(hours)], axis=1)
    innovation = (observed.reshape(1, -1) + 2.0 * spread * noise - flat) / (2.0 * spread)
    mean_pred = jnp.sum(pred_all, 0, keepdims=True) / members
    scaled_all = (pred_all - mean_pred) / (spread_root * (2.0 * spread))
    row_count = members + md
    extra = -row_count % (8 * basins)
    both = jnp.concatenate([scaled_all, innovation, jnp.zeros((extra, flat.shape[1]), f32)], 0)
    part = lax.dot_general(
        both, scaled_all, (((1,), (1,)), ((), ())),
        precision=exact_mode, preferred_element_type=f32,
    )
    sums = sum_over(part.reshape(basins, -1, members), "basin", 4).reshape(-1, members)
    gain = pl.pallas_call(
        functools.partial(solve_body, n_member, md),
        out_shape=jax.ShapeDtypeStruct((members, md), f32),
        in_specs=[vmem_spec()],
        out_specs=vmem_spec(),
        scratch_shapes=[VMEM((members, members), f32), VMEM((members, md), f32)],
        cost_estimate=pl.CostEstimate(
            flops=40_000_000, bytes_accessed=60_000_000, transcendentals=0
        ),
        name="solve",
    )(sums)

    mean_prior = jnp.sum(prior_all, 0, keepdims=True) / members
    anomaly = (prior_all - mean_prior) / spread_root
    change = lax.dot_general(
        gain, anomaly, (((0,), (0,)), ((), ())), precision=exact_mode, preferred_element_type=f32
    )
    posterior = prior_params + change.reshape(md, param_count, block_dev)
    return (posterior, predicted)


def solution(mesh):
    return jax.shard_map(
        shards,
        mesh=mesh,
        in_specs=(
            P("member", None, "basin"),
            P("member", None, "basin"),
            P("basin"),
            P("basin"),
            P("basin"),
            P("basin"),
            P("basin"),
            P(None, "basin"),
            P(None, "basin"),
            P("member", None, "basin"),
        ),
        out_specs=(P("member", None, "basin"), P("member", None, "basin")),
        check_vma=False,
    )
```

```python
import functools
import math

import jax
import jax.numpy as jnp
from jax import lax
import numpy as np
from jax.experimental import pallas as pl
from jax.experimental.pallas import tpu as pltpu
from jax.sharding import PartitionSpec as P

LANES = 128
BLK_LEV = 64
exact_mode = lax.Precision.HIGHEST
VMEM = pltpu.VMEM
SMEM = pltpu.SMEM
MESH = pl.DeviceIdType.MESH


def vmem_spec():
    return pl.BlockSpec(memory_space=VMEM)


def smem_spec():
    return pl.BlockSpec(memory_space=SMEM)


def exchange_body(axis, n, spread_out, x_ref, o_ref, send_sem, recv_sem, own_sem):
    me = lax.axis_index(axis)
    barrier = pltpu.get_barrier_semaphore()
    for i in range(1, n):
        pl.semaphore_signal(
            barrier, inc=1, device_id={axis: lax.rem(me + i, n)}, device_id_type=MESH
        )
    pl.semaphore_wait(barrier, n - 1)
    copies = []
    for i in range(1, n):
        peer = lax.rem(me + i, n)
        copies.append(
            pltpu.make_async_remote_copy(
                src_ref=x_ref.at[peer] if spread_out else x_ref,
                dst_ref=o_ref.at[me],
                send_sem=send_sem.at[i - 1],
                recv_sem=recv_sem.at[i - 1],
                device_id={axis: peer},
                device_id_type=MESH,
            )
        )
    for copy in copies:
        copy.start()
    own = pltpu.make_async_copy(x_ref.at[me] if spread_out else x_ref, o_ref.at[me], own_sem)
    own.start()
    own.wait()
    for copy in copies:
        copy.wait()


def exchange(x, axis, collective_id, spread_out=False):
    n = lax.axis_size(axis)
    shape = x.shape if spread_out else (n,) + x.shape
    return pl.pallas_call(
        functools.partial(exchange_body, axis, n, spread_out),
        out_shape=jax.ShapeDtypeStruct(shape, x.dtype),
        in_specs=[vmem_spec()],
        out_specs=vmem_spec(),
        scratch_shapes=[
            pltpu.SemaphoreType.DMA((n - 1,)),
            pltpu.SemaphoreType.DMA((n - 1,)),
            pltpu.SemaphoreType.DMA,
        ],
        compiler_params=pltpu.CompilerParams(collective_id=collective_id, has_side_effects=True),
        name=f"exchange_{collective_id}",
    )(x)


def doubling_bits(n):
    bits = []
    bit = n // 2
    while bit:
        bits.append(bit)
        bit //= 2
    return bits


def observed_body(
    hours, n_basin, n, x_ref, o_ref, land_ref, part_send, part_recv, send_sem, recv_sem
):
    basin = lax.axis_index("basin")
    me = lax.axis_index("member")
    partners = [me + bit * (1 - 2 * lax.rem(me // bit, 2)) for bit in doubling_bits(n)]
    barrier = pltpu.get_barrier_semaphore()
    for i in range(1, n_basin):
        pl.semaphore_signal(
            barrier, inc=1, device_id={"basin": lax.rem(basin + i, n_basin)}, device_id_type=MESH
        )
    for partner in partners:
        pl.semaphore_signal(barrier, inc=1, device_id={"member": partner}, device_id_type=MESH)
    pl.semaphore_wait(barrier, n_basin - 1 + len(partners))
    parts = []
    for i in range(1, n_basin):
        peer = lax.rem(basin + i, n_basin)
        parts.append(
            pltpu.make_async_remote_copy(
                src_ref=x_ref.at[peer], dst_ref=land_ref.at[i - 1],
                send_sem=part_send.at[i - 1], recv_sem=part_recv.at[i - 1],
                device_id={"basin": peer}, device_id_type=MESH,
            )
        )
    for copy in parts:
        copy.start()
    for copy in parts:
        copy.wait()
    flows = x_ref[basin]
    for i in range(1, n_basin):
        flows = flows + land_ref[i - 1]
    pred = inverse_sinh(flows)
    rows = o_ref.shape[1]
    gauges = x_ref.shape[2]
    for h in range(hours):
        o_ref[0, :, h * gauges : (h + 1) * gauges] = pred[h * rows : (h + 1) * rows]

    copies = {}
    for p in range(n):
        if p:
            copies[p].wait_recv()
        for k, partner in enumerate(partners):
            to = 2**k + p
            if p < 2**k:
                copies[to] = pltpu.make_async_remote_copy(
                    src_ref=o_ref.at[p], dst_ref=o_ref.at[to],
                    send_sem=send_sem.at[to - 1], recv_sem=recv_sem.at[to - 1],
                    device_id={"member": partner}, device_id_type=MESH,
                )
                copies[to].start()
    for p in range(1, n):
        copies[p].wait_send()


def observed_gather(parts, hours, collective_id):
    n = lax.axis_size("member")
    n_basin = lax.axis_size("basin")
    rows, gauges = parts.shape[1] // hours, parts.shape[2]
    return pl.pallas_call(
        functools.partial(observed_body, hours, n_basin, n),
        out_shape=jax.ShapeDtypeStruct((n, rows, hours * gauges), parts.dtype),
        in_specs=[vmem_spec()],
        out_specs=vmem_spec(),
        scratch_shapes=[
            VMEM((n_basin - 1,) + parts.shape[1:], parts.dtype),
            pltpu.SemaphoreType.DMA((n_basin - 1,)),
            pltpu.SemaphoreType.DMA((n_basin - 1,)),
            pltpu.SemaphoreType.DMA((n - 1,)),
            pltpu.SemaphoreType.DMA((n - 1,)),
        ],
        compiler_params=pltpu.CompilerParams(collective_id=collective_id, has_side_effects=True),
        name=f"observed_{collective_id}",
    )(parts)


def sum_body(axis, n, x_ref, o_ref, land_ref, sem1, sem2, sem3, sem4):
    me = lax.axis_index(axis)
    barrier = pltpu.get_barrier_semaphore()
    for i in range(1, n):
        pl.semaphore_signal(
            barrier, inc=1, device_id={axis: lax.rem(me + i, n)}, device_id_type=MESH
        )
    pl.semaphore_wait(barrier, n - 1)
    copies = []
    for i in range(1, n):
        peer = lax.rem(me + i, n)
        copies.append(
            pltpu.make_async_remote_copy(
                src_ref=x_ref.at[peer], dst_ref=land_ref.at[i - 1],
                send_sem=sem1.at[i - 1], recv_sem=sem2.at[i - 1],
                device_id={axis: peer}, device_id_type=MESH,
            )
        )
    for copy in copies:
        copy.start()
    for copy in copies:
        copy.wait()
    total = x_ref[me]
    for i in range(1, n):
        total = total + land_ref[i - 1]
    o_ref[me] = total
    copies = []
    for i in range(1, n):
        copies.append(
            pltpu.make_async_remote_copy(
                src_ref=o_ref.at[me], dst_ref=o_ref.at[me],
                send_sem=sem3.at[i - 1], recv_sem=sem4.at[i - 1],
                device_id={axis: lax.rem(me + i, n)}, device_id_type=MESH,
            )
        )
    for copy in copies:
        copy.start()
    for copy in copies:
        copy.wait()


def sum_over(x, axis, collective_id):
    n = lax.axis_size(axis)
    return pl.pallas_call(
        functools.partial(sum_body, axis, n),
        out_shape=jax.ShapeDtypeStruct(x.shape, x.dtype),
        in_specs=[vmem_spec()],
        out_specs=vmem_spec(),
        scratch_shapes=[VMEM((n - 1,) + x.shape[1:], x.dtype)]
        + [pltpu.SemaphoreType.DMA((n - 1,))] * 4,
        compiler_params=pltpu.CompilerParams(collective_id=collective_id, has_side_effects=True),
        name=f"sum_{collective_id}",
    )(x)


def permuted_step(held, axis, bit):
    n = lax.axis_size(axis)
    other = lax.ppermute(held, axis, [(i, i ^ bit) for i in range(n)])
    return jnp.concatenate([held, other], 0)


def route_body(
    seg_count, level_count, members, gauges, hours, param_count,
    basin_ref, down_ref, count_ref, gauge_row_ref, gauge_pack_ref,
    meta_ref, prior_ref, cos_ref, pin_ref, pout_ref, lat_hbm,
    out_ref,
    up_ref, flow_ref, row_ref, now_ref, back_ref, carry_ref, par_ref, raw_ref, ready_ref, sem,
):
    first = basin_ref[0]
    lev = BLK_LEV
    seg_blocks = level_count * lev
    rows = members
    packs = LANES // members
    shape = (rows, LANES)
    lane = lax.broadcasted_iota(jnp.int32, shape, 1)
    place = (lane // members) * members + lax.broadcasted_iota(jnp.int32, shape, 0)

    chunks = sem.shape[0]
    chunk_rows = seg_blocks * hours // chunks

    def fetch(c, m):
        span = pl.ds(c * chunk_rows, chunk_rows)
        return pltpu.make_async_copy(lat_hbm.at[m, span], raw_ref.at[span, m], sem.at[c, m])

    for c in range(chunks):
        for m in range(members):
            fetch(c, m).start()

    def clear(i, _):
        up_ref[i] = jnp.zeros((2 * rows, LANES), jnp.float32)
        return 0

    lax.fori_loop(0, 2 * lev, clear, 0, unroll=8)

    def turned(values):
        return jnp.concatenate([values] * packs, axis=0).T

    def coefficients(seg, _):
        storage = 0.02 + 0.1 * jax.nn.sigmoid(meta_ref[seg, :members, :])
        weighting = 0.2 * jax.nn.sigmoid(meta_ref[seg, members : 2 * members, :])
        den = storage * (1.0 - weighting) + 0.5
        span = pl.ds(pl.multiple_of(seg * seg_blocks, seg_blocks), seg_blocks)
        now_ref[span, :] = turned((0.5 - storage * weighting) / den)
        back_ref[span, :] = turned((0.5 + storage * weighting) / den)
        carry_ref[span, :] = turned((storage * (1.0 - weighting) - 0.5) / den)
        return 0

    lax.fori_loop(first, seg_count, coefficients, 0)
    for k in range(param_count - 2):
        par_ref[k] = turned(0.2 * prior_ref[:, 2 + k, :])

    def place_group(tiles):
        flat = jnp.concatenate(tiles, axis=0).T
        strips = [flat[q * rows : (q + 1) * rows] for q in range(packs)]
        made = []
        for i in range(packs):
            total = None
            for q in range(packs):
                shift = ((q - i) * members) % LANES
                piece = pltpu.roll(strips[q], shift, 1) if shift else strips[q]
                total = piece if total is None else jnp.where(lane // members == q, piece, total)
            made.append(total)
        return made

    def relayout(group, _):
        base = group * packs
        for h in range(hours):
            tiles = [raw_ref[(base + i) * hours + h] for i in range(packs)]
            for i, tile in enumerate(place_group(tiles)):
                ready_ref[base + i, h] = tile
        for n, ref in enumerate((pin_ref, pout_ref)):
            tiles = [
                jnp.broadcast_to(ref[pl.ds(base + i, 1), :], shape) for i in range(packs)
            ]
            for i, tile in enumerate(place_group(tiles)):
                ready_ref[base + i, hours + n] = tile
        return 0

    chunk_groups = seg_blocks // packs // chunks
    for c in range(chunks):
        for m in range(members):
            fetch(c, m).wait()
        lax.fori_loop(c * chunk_groups, (c + 1) * chunk_groups, relayout, 0, unroll=2)

    def sweep(seg, level, parity, own):
        def block(j, _):
            here = level * lev + j
            b = seg * seg_blocks + here
            live = place < count_ref[b]
            now = now_ref[pl.ds(b, 1), :]
            back = back_ref[pl.ds(b, 1), :]
            carry = carry_ref[pl.ds(b, 1), :]
            if own:
                expo = cos_ref[0] * par_ref[0, pl.ds(here, 1), :]
                for k in range(1, cos_ref.shape[0]):
                    expo = expo + cos_ref[k] * par_ref[k, pl.ds(here, 1), :]
                scale = jnp.exp(expo)
                add0 = ready_ref[here, 0] * scale
                add1 = ready_ref[here, 1] * scale
                if level > 0:
                    add0 = add0 + up_ref[parity * lev + j, :rows]
                    add1 = add1 + up_ref[parity * lev + j, rows:]
                in0 = jnp.where(live, add0, 0.0)
                in1 = jnp.where(live, add1, 0.0)
                start = back * ready_ref[here, 2] + carry * ready_ref[here, 3]
                out0 = now * in0 + jnp.where(live, start, 0.0)
            else:
                in0 = jnp.where(live, up_ref[parity * lev + j, :rows], 0.0)
                in1 = jnp.where(live, up_ref[parity * lev + j, rows:], 0.0)
                out0 = now * in0
            out1 = now * in1 + back * in0 + carry * out0
            up_ref[parity * lev + j] = jnp.zeros((2 * rows, LANES), jnp.float32)
            flow_ref[pl.ds(here * 2 * rows, rows), :] = out0
            flow_ref[pl.ds(here * 2 * rows + rows, rows), :] = out1
            target = (1 - parity) * lev + down_ref[b]
            up_ref[target, :rows] += out0
            up_ref[target, rows:] += out1
            return 0

        lax.fori_loop(0, lev, block, 0, unroll=4)

    fold = lax.broadcasted_iota(jnp.int32, shape, 0) == lane % members
    fold = fold.astype(jnp.float32)
    one_lane = lax.broadcasted_iota(jnp.int32, (1, LANES), 1) // members

    def observe(seg):
        first_gauge = seg * gauges

        def one(g, _):
            row = gauge_row_ref[first_gauge + g]
            keep = one_lane == gauge_pack_ref[first_gauge + g]
            row_ref[pl.ds(g, 1), :] = jnp.where(keep, flow_ref[pl.ds(row, 1), :], 0.0)
            row_ref[pl.ds(gauges + g, 1), :] = jnp.where(
                keep, flow_ref[pl.ds(row + rows, 1), :], 0.0
            )
            return 0

        lax.fori_loop(0, gauges, one, 0, unroll=8)
        for h in range(2):
            out_ref[seg, h * members : (h + 1) * members, :] = lax.dot_general(
                fold, row_ref[h * gauges : (h + 1) * gauges, :], (((1,), (1,)), ((), ())),
                precision=exact_mode, preferred_element_type=jnp.float32,
            )

    def nothing(seg, _):
        out_ref[seg] = jnp.zeros(out_ref.shape[1:], jnp.float32)
        return 0

    lax.fori_loop(0, first, nothing, 0)
    for level in range(level_count):
        sweep(first, level, level % 2, True)
    observe(first)

    def later(seg, _):
        for level in range(level_count):
            sweep(seg, level, level % 2, False)
        observe(seg)
        return 0

    lax.fori_loop(first + 1, seg_count, later, 0)


def invert_small(d, panel=8):
    size = d.shape[0]
    lane = lax.broadcasted_iota(jnp.int32, d.shape, 1)
    sub = lax.broadcasted_iota(jnp.int32, d.shape, 0)
    for base in range(0, size, panel):
        cols = [jnp.broadcast_to(d[:, base + i : base + i + 1], d.shape) for i in range(panel)]
        for i in range(panel):
            j = base + i
            pivot = cols[i]
            inv = 1.0 / pivot[j : j + 1, :]
            row = jnp.where(lane[:1] == j, 1.0, d[j : j + 1, :]) * inv
            d = jnp.where(sub == j, row, jnp.where(lane == j, 0.0, d) - pivot * row)
            for l in range(i + 1, panel):
                factor = pivot[base + l : base + l + 1, :] * inv
                cols[l] = jnp.where(sub == j, factor, cols[l] - pivot * factor)
    return d


def exact_dot(a, b):
    return jnp.dot(a, b, precision=exact_mode, preferred_element_type=jnp.float32)


def solve_body(n, size, sums_ref, out_ref, a_ref, l_ref):
    total = n * size
    sub = lax.broadcasted_iota(jnp.int32, (total, total), 0)
    lane = lax.broadcasted_iota(jnp.int32, (total, total), 1)
    a_ref[...] = sums_ref[:total, :] + jnp.where(lane == sub, 1.0, 0.0)
    out_ref[...] = sums_ref[total : total + size, :].T
    for k in range(n):
        span = slice(k * size, (k + 1) * size)
        left = (k * size // LANES) * LANES
        inverse = invert_small(a_ref[span, span])
        right = exact_dot(inverse, out_ref[span, :])
        l_ref[...] = a_ref[:, span]
        l_ref[span, :] = jnp.zeros((size, size), jnp.float32)
        column = l_ref[...]
        if k < n - 1:
            top = exact_dot(inverse, a_ref[span, left:])
            a_ref[:, left:] -= exact_dot(column, top)
            a_ref[span, left:] = top
        out_ref[...] -= exact_dot(column, right)
        out_ref[span, :] = right


def inverse_sinh(values):
    return jnp.log(values + jnp.sqrt(values * values + 1.0))


def shards(
    prior_params, lateral_flow, inflow_start, outflow_start, reach_count, downstream,
    gauge_reach, observed, obs_var, obs_noise,
):
    md, param_count, block_dev = prior_params.shape
    hours = lateral_flow.shape[1]
    gauges = gauge_reach.shape[0]
    basins = lax.axis_size("basin")
    n_member = lax.axis_size("member")
    members = md * n_member
    level_count = block_dev // BLK_LEV
    packs = LANES // md
    f32 = jnp.float32

    prior_steps = doubling_bits(n_member)
    held = permuted_step(prior_params[None], "member", prior_steps[0])

    gauge_rows = gauges // block_dev
    extra = -(md * 2 + 2 + gauge_rows) % 8
    meta = jnp.concatenate(
        [
            prior_params[:, 0, :],
            prior_params[:, 1, :],
            downstream.astype(f32)[None],
            reach_count.astype(f32)[None],
            gauge_reach.astype(f32).reshape(-1, block_dev),
            jnp.zeros((extra, block_dev), f32),
        ],
        0,
    )
    meta_all = exchange(meta, "basin", 1)
    down_all = meta_all[:, md * 2].reshape(-1).astype(jnp.int32)
    count_all = meta_all[:, md * 2 + 1].reshape(-1).astype(jnp.int32)
    slots = meta_all[:, md * 2 + 2 : md * 2 + 2 + gauge_rows].reshape(-1).astype(jnp.int32)
    gauge_row = slots // LANES * (hours * md) + slots % md
    gauge_pack = slots % LANES // md

    modes = param_count - 2
    lane_pos = np.arange(LANES)
    cosine = np.cos(math.pi * np.arange(modes)[:, None] * (lane_pos[None, :] + 0.5) / LANES)
    cosine = np.swapaxes(cosine.reshape(modes, packs, md), 1, 2)
    cosine = jnp.asarray(np.repeat(cosine, md, axis=2), f32)

    lateral = lateral_flow.reshape(md, hours, block_dev, LANES)
    lateral = jnp.swapaxes(lateral, 1, 2).reshape(md, block_dev * hours, LANES)
    held, meta_all = lax.optimization_barrier((held, meta_all))
    for bit in prior_steps[1:-1]:
        held = permuted_step(held, "member", bit)
    basin_idx = lax.axis_index("basin").astype(jnp.int32).reshape(1)
    seg_coef = VMEM((basins * block_dev, LANES), f32)

    parts = pl.pallas_call(
        functools.partial(route_body, basins, level_count, md, gauges, hours, param_count),
        out_shape=jax.ShapeDtypeStruct((basins, 2 * md, gauges), f32),
        in_specs=[smem_spec()] * 5 + [vmem_spec()] * 5 + [pl.BlockSpec(memory_space=pl.ANY)],
        out_specs=vmem_spec(),
        scratch_shapes=[
            VMEM((2 * BLK_LEV, 2 * md, LANES), f32),
            VMEM((block_dev * 2 * md, LANES), f32),
            VMEM((2 * gauges, LANES), f32),
            seg_coef,
            seg_coef,
            seg_coef,
            VMEM((modes, block_dev, LANES), f32),
            VMEM((block_dev * hours, md, LANES), f32),
            VMEM((block_dev, hours + 2, md, LANES), f32),
            pltpu.SemaphoreType.DMA((4, md)),
        ],
        cost_estimate=pl.CostEstimate(
            flops=40_000_000, bytes_accessed=60_000_000, transcendentals=0
        ),
        name="route",
    )(
        basin_idx, down_all, count_all, gauge_row, gauge_pack, meta_all, prior_params, cosine,
        inflow_start.reshape(block_dev, LANES), outflow_start.reshape(block_dev, LANES), lateral,
    )
    parts, held = lax.optimization_barrier((parts, held))
    held = permuted_step(held, "member", prior_steps[-1])
    prior_all = held.reshape(members, param_count * block_dev)
    gathered = observed_gather(parts, hours, 2)
    flat = gathered[0]
    predicted = flat.reshape(md, hours, gauges)
    pred_all = gathered.reshape(members, hours * gauges)

    spread = jnp.sqrt(obs_var).reshape(1, -1)
    spread_root = math.sqrt(members - 1.0)
    noise = jnp.concatenate([obs_noise[:, h] for h in range(hours)], axis=1)
    innovation = (observed.reshape(1, -1) + 2.0 * spread * noise - flat) / (2.0 * spread)
    mean_pred = jnp.sum(pred_all, 0, keepdims=True) / members
    scaled_all = (pred_all - mean_pred) / (spread_root * (2.0 * spread))
    row_count = members + md
    extra = -row_count % (8 * basins)
    both = jnp.concatenate([scaled_all, innovation, jnp.zeros((extra, flat.shape[1]), f32)], 0)
    part = lax.dot_general(
        both, scaled_all, (((1,), (1,)), ((), ())),
        precision=exact_mode, preferred_element_type=f32,
    )
    sums = sum_over(part.reshape(basins, -1, members), "basin", 4).reshape(-1, members)
    gain = pl.pallas_call(
        functools.partial(solve_body, n_member, md),
        out_shape=jax.ShapeDtypeStruct((members, md), f32),
        in_specs=[vmem_spec()],
        out_specs=vmem_spec(),
        scratch_shapes=[VMEM((members, members), f32), VMEM((members, md), f32)],
        cost_estimate=pl.CostEstimate(
            flops=40_000_000, bytes_accessed=60_000_000, transcendentals=0
        ),
        name="solve",
    )(sums)

    mean_prior = jnp.sum(prior_all, 0, keepdims=True) / members
    anomaly = (prior_all - mean_prior) / spread_root
    change = lax.dot_general(
        gain, anomaly, (((0,), (0,)), ((), ())), precision=exact_mode, preferred_element_type=f32
    )
    posterior = prior_params + change.reshape(md, param_count, block_dev)
    return (posterior, predicted)


def solution(mesh):
    return jax.shard_map(
        shards,
        mesh=mesh,
        in_specs=(
            P("member", None, "basin"),
            P("member", None, "basin"),
            P("basin"),
            P("basin"),
            P("basin"),
            P("basin"),
            P("basin"),
            P(None, "basin"),
            P(None, "basin"),
            P("member", None, "basin"),
        ),
        out_specs=(P("member", None, "basin"), P("member", None, "basin")),
        check_vma=False,
    )
```
